32 devices in a mesh: segment: 2 (over x), rows: 4 (over y, core), cols: 4 (over z).
Axes of the slice: x: 2, y: 2, z: 4, core: 2. Of those that a mesh axis runs over, the one named last changes fastest.
Arguments:
- measure: bfloat16 [512, 4096], P('rows', 'cols'), may hold values from -6 to 6
- aperture: int32 [512, 4096], P('rows', 'cols'), may hold values 0 or 1
- shifts: int32 [28], replicated, may hold values from 0 to 54, as said below
- target: bfloat16 [28, 512, 4096], P(None, 'rows', 'cols'), may hold values from -6 to 6
- enc_weight: bfloat16 [128, 28, 4, 4], replicated, may hold values from -0.25 to 0.25
- proj_weight: bfloat16 [48, 128], replicated, may hold values from -0.5 to 0.5
- in_weight: bfloat16 [3, 3, 48, 28], replicated, may hold values from -0.375 to 0.375
- out_weight: bfloat16 [28, 48], replicated, may hold values from -0.875 to 0.875
Outputs:
- recon: bfloat16 [28, 512, 4096], P('segment', 'rows', 'cols')
- grad_enc: float32 [128, 28, 4, 4], replicated
- grad_proj: float32 [48, 128], replicated
- grad_in: float32 [3, 3, 48, 28], replicated
- grad_out: float32 [28, 48], replicated
The draws below stay inside these ranges and needn't reach their ends.
Inputs may be any that keep to these rules, and one draw needn't show every extreme that they name: shifts[0] is 0, shifts[27] is 54, and the shifts never fall from one band to the next.
All inputs are finite; a program needn't handle non-finite values. No bound on the sum of `aperture` on one device may be relied on, other than what follows from the above.
Results may differ from the reference program's by a relative error of at most 0.0055.
Values may be sent and summed in bfloat16 or wider, within the bound.
No kernel may reach another device: no remote copies, remote signals or barrier semaphores. Data moves between devices by JAX's collectives and lax.ppermute only.
A program may use at most 384 MiB of HBM per device.

```python
import jax
import jax.numpy as jnp
from jax import lax

L = 28
CC = 128
CF = 48
FR = 128
SMAX = 54
H = 512
W = 4096
N_ROWS = 4


def draw_shifts(key, part):
    band_index = jnp.arange(L, dtype=jnp.int32)
    wobble = jax.random.randint(key, (L,), -1, 2, dtype=jnp.int32)
    wobble = jnp.where((band_index == 0) | (band_index == L - 1), 0, wobble)
    return jnp.clip(2 * band_index + wobble, 0, SMAX).astype(jnp.int32)


def set_ends(result, key, smallest, largest):
    place = [jax.random.randint(jax.random.fold_in(key, axis), (), 0, length) for axis, length in enumerate(result.shape)]
    longest = result.shape.index(max(result.shape))
    beside = place[:longest] + [(place[longest] + 1) % result.shape[longest]] + place[longest + 1:]
    return result.at[tuple(place)].set(smallest).at[tuple(beside)].set(largest)


def block_scale(rng, dims, cuts, least, top_value):
    gain, own = 1.0, jax.random.fold_in(rng, 6)
    for dim, parts in cuts:
        heights = jnp.exp(jax.random.uniform(jax.random.fold_in(own, dim), (parts,), jnp.float32, least / len(cuts), top_value / len(cuts)))
        gain = gain * jnp.repeat(heights, dims[dim] // parts).reshape([-1 if axis == dim else 1 for axis in range(len(dims))])
    return gain


def bell_draw(own_key, dims, scale, reach, split=(), kind=jnp.bfloat16):
    level = block_scale(own_key, dims, split, -0.22, 0.18) if split else 1.0
    values = jax.random.normal(own_key, dims, jnp.float32) * scale * level
    return jnp.minimum(jnp.maximum(values, -reach), reach).astype(kind)


def setup_inputs(seed: int = 0) -> dict:
    key_of = jax.random.split(jax.random.key(seed), 9)
    measure = bell_draw(key_of[0], (H, W), 1.0, 6.0, ((0, 4), (1, 4)))
    aperture = set_ends((jax.random.randint(key_of[1], (H, W), 0, 2) < 1).astype(jnp.int32), jax.random.fold_in(key_of[1], 1), 0, 1)
    shifts = draw_shifts(jax.random.fold_in(key_of[8], 71), 0)
    target = bell_draw(key_of[3], (L, H, W), 1.0, 6.0, ((1, 4), (2, 4)))
    enc_weight = bell_draw(key_of[4], (CC, L, 4, 4), (16 * L) ** -0.5, 0.25)
    proj_weight = bell_draw(key_of[5], (CF, CC), CC ** -0.5, 0.5)
    in_weight = bell_draw(key_of[6], (3, 3, CF, L), (9 * L) ** -0.5, 0.375)
    out_weight = bell_draw(key_of[7], (L, CF), CF ** -0.5, 0.875)
    return dict(measure=measure, aperture=aperture, shifts=shifts, target=target, enc_weight=enc_weight, proj_weight=proj_weight, in_weight=in_weight, out_weight=out_weight)


def silu_slope(value):
    sigma = jax.nn.sigmoid(value)
    return sigma * (1.0 + value * (1.0 - sigma))

def widen(coarse):
    channels, coarse_rows, coarse_cols = coarse.shape
    spread = jnp.broadcast_to(coarse[:, :, None, :, None], (channels, coarse_rows, 4, coarse_cols, 4))
    return spread.reshape(channels, coarse_rows * 4, coarse_cols * 4)

def spatial(padded, weight, tile_rows, tile_cols):
    total = jnp.zeros((weight.shape[2], tile_rows, tile_cols), jnp.float32)
    for a in range(3):
        for b in range(3):
            window = padded[:, a:a + tile_rows, b:b + tile_cols].astype(jnp.float32)
            total = total + jnp.einsum('fk,krc->frc', weight[a, b].astype(jnp.float32), window)
    return total

def kernel_grad(grad, padded, tile_rows, tile_cols):
    grad_wide = grad.astype(jnp.float32)
    outer = []
    for a in range(3):
        inner = []
        for b in range(3):
            window = padded[:, a:a + tile_rows, b:b + tile_cols].astype(jnp.float32)
            inner.append(jnp.einsum('frc,krc->fk', grad_wide, window))
        outer.append(jnp.stack(inner))
    return jnp.stack(outer)

def reference(measure, aperture, shifts, target, enc_weight, proj_weight, in_weight, out_weight):
    height, width = measure.shape
    bands = shifts.shape[0]
    pixels = float(height * width)
    extended = jnp.pad(measure, ((0, 0), (0, SMAX)))
    initial = jax.vmap(lambda offset: lax.dynamic_slice_in_dim(extended, offset.astype(jnp.int32), width, 1))(shifts.astype(jnp.int32))
    initial = initial * aperture.astype(measure.dtype)[None]
    patches = initial.reshape(bands, height // 4, 4, width // 4, 4)
    encoded = jnp.einsum('okab,kpaqb->opq', enc_weight.astype(jnp.float32), patches.astype(jnp.float32))
    features = jax.nn.silu(encoded).astype(jnp.bfloat16)
    projected = jnp.einsum('fo,opq->fpq', proj_weight.astype(jnp.float32), features.astype(jnp.float32)).astype(jnp.bfloat16)
    bordered = jnp.pad(initial, ((0, 0), (1, 1), (1, 1)))
    zero = jnp.zeros((), jnp.int32)

    def strip(carry, index):
        grad_in, grad_out = carry
        start = (index * FR).astype(jnp.int32)
        coarse_start = (index * (FR // 4)).astype(jnp.int32)
        local = lax.dynamic_slice(bordered, (zero, start, zero), (bands, FR + 2, width + 2))
        coarse = lax.dynamic_slice(projected, (zero, coarse_start, zero), (CF, FR // 4, width // 4))
        truth = lax.dynamic_slice(target, (zero, start, zero), (bands, FR, width))
        own = local[:, 1:-1, 1:-1]
        pre_act = spatial(local, in_weight, FR, width) + widen(coarse).astype(jnp.float32)
        hidden = jax.nn.silu(pre_act).astype(jnp.bfloat16)
        recon = (own.astype(jnp.float32) + jnp.einsum('kf,frc->krc', out_weight.astype(jnp.float32), hidden.astype(jnp.float32))).astype(jnp.bfloat16)
        residual_grad = ((recon.astype(jnp.float32) - truth.astype(jnp.float32)) / pixels).astype(jnp.bfloat16)
        grad_out = grad_out + jnp.einsum('krc,frc->kf', residual_grad.astype(jnp.float32), hidden.astype(jnp.float32))
        hidden_grad = jnp.einsum('kf,krc->frc', out_weight.astype(jnp.float32), residual_grad.astype(jnp.float32))
        pre_grad = (hidden_grad * silu_slope(pre_act)).astype(jnp.bfloat16)
        grad_in = grad_in + kernel_grad(pre_grad, local, FR, width)
        adjoint = lax.optimization_barrier(jnp.sum(pre_grad.astype(jnp.float32).reshape(CF, FR // 4, 4, width // 4, 4), axis=(2, 4))).astype(jnp.bfloat16)
        return ((grad_in, grad_out), (recon, adjoint))
    start_carry = (jnp.zeros(in_weight.shape, jnp.float32), jnp.zeros(out_weight.shape, jnp.float32))
    (grad_in, grad_out), (recon_blocks, adjoint_blocks) = lax.scan(strip, start_carry, jnp.arange(N_ROWS, dtype=jnp.int32))
    recon = jnp.moveaxis(recon_blocks, 0, 1).reshape(bands, height, width)
    coarse_adj = jnp.moveaxis(adjoint_blocks, 0, 1).reshape(CF, height // 4, width // 4)
    grad_proj = jnp.einsum('fpq,opq->fo', coarse_adj.astype(jnp.float32), features.astype(jnp.float32))
    feat_grad = jnp.einsum('fo,fpq->opq', proj_weight.astype(jnp.float32), coarse_adj.astype(jnp.float32)).astype(jnp.bfloat16)
    enc_grad_pre = (feat_grad.astype(jnp.float32) * silu_slope(encoded)).astype(jnp.bfloat16)
    grad_enc = jnp.einsum('opq,kpaqb->okab', enc_grad_pre.astype(jnp.float32), patches.astype(jnp.float32))
    return (recon, grad_enc, grad_proj, grad_in, grad_out)
```

```python
import functools
import jax
import jax.numpy as jnp
from jax import lax
from jax.experimental import pallas as pl
from jax.experimental.pallas import tpu as pltpu
from jax.sharding import PartitionSpec as P

AXES = ("segment", "rows", "cols")
BP = 32
CW = 256
STEP = 16
GROWS = 768


def nt(x, y):
    return lax.dot_general(x, y, (((1,), (1,)), ((), ())), preferred_element_type=jnp.float32)


def mm(x, y):
    return jnp.dot(x, y, preferred_element_type=jnp.float32)


def pixel_kernel(
    shifts_ref, place_ref, field_ref, *refs,
    backward, half_rows, cols, bands, fine, chan, inv_pixels, own,
):
    if backward:
        (target_ref, wenc_ref, wproj_ref, wprojt_ref, win_ref, wout_ref, woutt_ref,
         recon_ref, grad_ref, x3, tmp, spread, gather, widen, fold, wide, patch, rtmp,
         ttmp, feat_s, slope_s, pgrad, gin, gout) = refs
    else:
        (wenc_ref, wproj_ref, win_ref, wout_ref, _, recon_ref,
         x3, tmp, gather, widen, wide, patch, rtmp) = refs
    step = pl.program_id(0)
    half = place_ref[0]
    first_band = place_ref[1]
    ext = cols + 128
    slab = 3 * BP
    quart = cols // 4

    @pl.when(step == 0)
    def _():
        row = lax.broadcasted_iota(jnp.int32, (512, 512), 0)
        col = lax.broadcasted_iota(jnp.int32, (512, 512), 1)
        gather[...] = (row == 4 * (col % 128) + col // 128).astype(jnp.bfloat16)
        row = lax.broadcasted_iota(jnp.int32, (128, 512), 0)
        col = lax.broadcasted_iota(jnp.int32, (128, 512), 1)
        widen[...] = (row == col // 4).astype(jnp.bfloat16)
        tmp[...] = jnp.zeros_like(tmp)
        if backward:
            row = lax.broadcasted_iota(jnp.int32, (512, 128), 0)
            col = lax.broadcasted_iota(jnp.int32, (512, 128), 1)
            fold[...] = (row // 4 == col).astype(jnp.bfloat16)
            ttmp[...] = jnp.zeros_like(ttmp)
            grad_ref[...] = jnp.zeros_like(grad_ref)
            gin[...] = jnp.zeros_like(gin)
            gout[...] = jnp.zeros_like(gout)

    def build(group):
        start = pl.multiple_of(half * half_rows + 8 * group, 8)
        meas = field_ref[0, pl.ds(start, 8), :]
        aper = field_ref[1, pl.ds(start, 8), :]
        for k in range(bands):
            s = shifts_ref[k]
            rolled = pltpu.roll(meas, jnp.where(s == 0, 0, ext - s), 1)
            val = rolled * aper
            for t in range(ext // 128):
                tmp[t, pl.ds(k, 8, stride=BP), :] = val[:, 128 * t:128 * t + 128]

        def pack(r, _):
            base = pl.multiple_of(r * BP, BP)
            mid = jnp.concatenate([tmp[t, pl.ds(base, BP), :] for t in range(ext // 128)], axis=1)
            left = pltpu.roll(mid, 1, 1)[:, :cols]
            right = pltpu.roll(mid, ext - 1, 1)[:, :cols]
            dst = pl.multiple_of((8 * group + r) * slab, slab)
            x3[pl.ds(dst, BP), :] = left.astype(jnp.bfloat16)
            x3[pl.ds(dst + BP, BP), :] = mid[:, :cols].astype(jnp.bfloat16)
            x3[pl.ds(dst + 2 * BP, BP), :] = right.astype(jnp.bfloat16)
            return 0

        lax.fori_loop(0, 8, pack, 0)

    @pl.when(step == 0)
    def _():
        def body(g, _):
            build(g)
            return 0
        lax.fori_loop(0, 4, body, 0)

    @pl.when(step > 0)
    def _():
        def body(g, _):
            build(2 * step + 2 + g)
            return 0
        lax.fori_loop(0, 2, body, 0)

    if backward:
        for k in range(bands):
            ttmp_val = target_ref[k].astype(jnp.float32)
            for t in range(cols // 128):
                ttmp[t, k * STEP:(k + 1) * STEP, :] = ttmp_val[:, 128 * t:128 * t + 128]

    def coarse(p, _):
        base = step * STEP + 4 * p + 8
        for cg in range(quart // 128):
            rows4 = jnp.concatenate(
                [x3[pl.ds(pl.multiple_of((base + a) * slab + BP, BP), BP), 512 * cg:512 * cg + 512]
                 for a in range(4)], axis=0)
            out = mm(rows4, gather[...]).astype(jnp.bfloat16)
            for b in range(4):
                patch[b * 4 * BP:(b + 1) * 4 * BP, 128 * cg:128 * cg + 128] = out[:, 128 * b:128 * b + 128]
        encoded = mm(wenc_ref[...], patch[...])
        sig = 0.5 * jnp.tanh(0.5 * encoded) + 0.5
        silu = encoded * sig
        feat = silu.astype(jnp.bfloat16)
        if backward:
            feat_s[...] = feat
            slope_s[...] = sig + silu * (1.0 - sig)
        proj = mm(wproj_ref[...], feat).astype(jnp.bfloat16)
        for cg in range(quart // 128):
            wide[:, 512 * cg:512 * cg + 512] = mm(proj[:, 128 * cg:128 * cg + 128], widen[...])
        for r in range(4):
            win0 = pl.multiple_of((base + r - 1) * slab, slab)
            line = 4 * p + r
            for c in range(cols // CW):
                lanes = slice(CW * c, CW * c + CW)
                pre = mm(win_ref[...], x3[pl.ds(win0, 3 * slab), lanes]) + wide[:, lanes]
                sig = 0.5 * jnp.tanh(0.5 * pre) + 0.5
                silu = pre * sig
                hid = silu.astype(jnp.bfloat16)
                est = x3[pl.ds(win0 + slab + BP, BP), lanes].astype(jnp.float32)
                rec = (est + mm(wout_ref[...], hid)).astype(jnp.bfloat16)
                recf = rec.astype(jnp.float32)
                for t in range(CW // 128):
                    rtmp[c * (CW // 128) + t, pl.ds(line, BP, stride=STEP), :] = recf[:, 128 * t:128 * t + 128]
                if backward:
                    truth = jnp.concatenate(
                        [ttmp[c * (CW // 128) + t, pl.ds(line, BP, stride=STEP), :]
                         for t in range(CW // 128)], axis=1)
                    res = ((recf - truth) * inv_pixels).astype(jnp.bfloat16)
                    gout[...] += nt(res, hid)
                    hgrad = mm(woutt_ref[...], res)
                    pg = (hgrad * (sig + silu * (1.0 - sig))).astype(jnp.bfloat16)
                    pgrad[r * fine:(r + 1) * fine, lanes] = pg
            if backward:
                gin[...] += nt(pgrad[r * fine:(r + 1) * fine, :], x3[pl.ds(win0, 3 * slab), :])
        if backward:
            parts = []
            for cg in range(quart // 128):
                tot = mm(pgrad[:, 512 * cg:512 * cg + 512], fold[...])
                parts.append(tot[:fine] + tot[fine:2 * fine] + tot[2 * fine:3 * fine] + tot[3 * fine:])
            cadj = jnp.concatenate(parts, axis=1).astype(jnp.bfloat16)
            grad_ref[512:512 + fine, :] += nt(cadj, feat_s[...])
            fg = mm(wprojt_ref[...], cadj).astype(jnp.bfloat16)
            egp = (fg.astype(jnp.float32) * slope_s[...]).astype(jnp.bfloat16)
            grad_ref[0:512, :] += nt(patch[...], egp)
        return 0

    lax.fori_loop(0, STEP // 4, coarse, 0)

    for kk in range(own):
        src = pl.multiple_of((first_band + kk) * STEP, STEP)
        for t in range(cols // 128):
            recon_ref[kk, :, 128 * t:128 * t + 128] = rtmp[t, pl.ds(src, STEP), :].astype(jnp.bfloat16)

    if backward:
        @pl.when(step == pl.num_programs(0) - 1)
        def _():
            for t in range(3):
                w = min(128, 3 * slab - 128 * t)
                grad_ref[560 + t * fine:560 + (t + 1) * fine, 0:w] = gin[:, 128 * t:128 * t + w]
            grad_ref[560 + 3 * fine:560 + 3 * fine + BP, 0:fine] = gout[...]


def run_half(shifts, place, field, target, weights, recon, *, backward, pixels, own):
    rows2, ext = field.shape[1:]
    cols = ext - 128
    tile_rows = rows2 - 16
    half_rows = tile_rows // 2
    bands = shifts.shape[0]
    wenc, wproj, win, wout = weights
    chan, fine = wenc.shape[0], wproj.shape[0]
    steps = half_rows // STEP
    whole = lambda shape: pl.BlockSpec(shape, lambda i, *_: (0,) * len(shape))
    strip = lambda n: pl.BlockSpec((n, STEP, cols), lambda i, sh, pc: (0, pc[0] * steps + i, 0))
    slots = half_rows + 16
    f32, bf16 = jnp.float32, jnp.bfloat16
    x3 = pltpu.VMEM((slots * 3 * BP, cols), bf16)
    tmp = pltpu.VMEM((ext // 128, 8 * BP, 128), f32)
    gather = pltpu.VMEM((512, 512), bf16)
    widen = pltpu.VMEM((128, 512), bf16)
    wide = pltpu.VMEM((fine, cols), f32)
    patch = pltpu.VMEM((16 * BP, cols // 4), bf16)
    rtmp = pltpu.VMEM((cols // 128, BP * STEP, 128), f32)
    recon_shape = jax.ShapeDtypeStruct((own, tile_rows, cols), bf16)
    body = functools.partial(
        pixel_kernel, backward=backward, half_rows=half_rows, cols=cols, bands=bands, fine=fine,
        chan=chan, inv_pixels=1.0 / pixels, own=own)
    if backward:
        ops = (field, target, wenc, wproj, wproj.T, win, wout, wout.T)
        in_specs = [whole(field.shape), strip(bands)] + [whole(x.shape) for x in ops[2:]]
        out_shape = (recon_shape, jax.ShapeDtypeStruct((GROWS, 128), f32))
        out_specs = (strip(own), whole((GROWS, 128)))
        scratch = [x3, tmp, pltpu.VMEM((8, 128), f32), gather, widen, pltpu.VMEM((512, 128), bf16), wide, patch, rtmp,
                   pltpu.VMEM((cols // 128, BP * STEP, 128), f32), pltpu.VMEM((chan, cols // 4), bf16),
                   pltpu.VMEM((chan, cols // 4), f32), pltpu.VMEM((4 * fine, cols), bf16),
                   pltpu.VMEM((fine, 9 * BP), f32), pltpu.VMEM((BP, fine), f32)]
        alias = {}
    else:
        ops = (field, wenc, wproj, win, wout, recon)
        in_specs = [whole(x.shape) for x in ops[:5]] + [pl.BlockSpec(memory_space=pl.ANY)]
        out_shape = recon_shape
        out_specs = strip(own)
        scratch = [x3, tmp, gather, widen, wide, patch, rtmp]
        alias = {7: 0}
    return pl.pallas_call(
        body,
        out_shape=out_shape,
        grid_spec=pltpu.PrefetchScalarGridSpec(
            num_scalar_prefetch=2, grid=(steps,), in_specs=in_specs, out_specs=out_specs,
            scratch_shapes=scratch),
        compiler_params=pltpu.CompilerParams(
            dimension_semantics=("arbitrary",), vmem_limit_bytes=60 << 20),
        input_output_aliases=alias,
        name="grad_half" if backward else "recon_half",
    )(shifts, place, *ops)


def moved(x, axis, by):
    n = lax.axis_size(axis)
    return lax.ppermute(x, axis, [(i, i + by) for i in range(n) if 0 <= i + by < n])


def bordered(measure, aperture):
    pair = jnp.stack([measure, aperture.astype(jnp.bfloat16)])
    right = moved(pair[:, :, :64], "cols", -1)
    left = moved(pair[:, :, -64:], "cols", 1)
    wide = jnp.concatenate([pair, right, left], axis=2)
    above = moved(wide[:, -8:], "rows", 1)
    below = moved(wide[:, :8], "rows", -1)
    return jnp.concatenate([above, wide, below], axis=1).astype(jnp.float32)


def pack_weights(enc_weight, proj_weight, in_weight, out_weight):
    bands = out_weight.shape[0]
    pad = BP - bands
    enc = jnp.pad(enc_weight.transpose(0, 3, 2, 1), ((0, 0), (0, 0), (0, 0), (0, pad)))
    enc = enc.reshape(enc.shape[0], -1)
    inw = jnp.pad(in_weight.transpose(2, 0, 1, 3), ((0, 0), (0, 0), (0, 0), (0, pad)))
    inw = inw.reshape(inw.shape[0], -1)
    out = jnp.pad(out_weight, ((0, pad), (0, 0)))
    return enc, proj_weight, inw, out


def unpack(total, bands, fine, chan):
    enc = total[:512].reshape(4, 4, BP, chan)[:, :, :bands].transpose(3, 2, 1, 0)
    proj = total[512:512 + fine]
    gin = total[560:560 + 3 * fine].reshape(3, fine, 128).transpose(1, 0, 2).reshape(fine, 384)
    gin = gin[:, :9 * BP].reshape(fine, 3, 3, BP)[..., :bands].transpose(1, 2, 0, 3)
    out = total[560 + 3 * fine:560 + 3 * fine + bands, :fine]
    return enc, proj, gin, out


def all_sum(grad):
    n = lax.axis_size(AXES)
    mine = lax.all_to_all(grad.reshape(n, GROWS // n, 128), AXES, 0, 0, tiled=True)
    mine = jnp.sum(mine, axis=0)
    every = lax.all_to_all(jnp.broadcast_to(mine, (n,) + mine.shape), AXES, 0, 0, tiled=True)
    return every.reshape(GROWS, 128)


def per_device(measure, aperture, shifts, target, enc_weight, proj_weight, in_weight, out_weight):
    tile_rows, tile_cols = measure.shape
    bands = shifts.shape[0]
    pixels = float(tile_rows * lax.axis_size("rows") * tile_cols * lax.axis_size("cols"))
    seg = lax.axis_index("segment")
    own = bands // lax.axis_size("segment")
    field = bordered(measure, aperture)
    weights = pack_weights(enc_weight, proj_weight, in_weight, out_weight)
    place = jnp.stack([seg, seg * own]).astype(jnp.int32)
    other = jnp.stack([1 - seg, seg * own]).astype(jnp.int32)
    recon, grad = run_half(shifts, place, field, target, weights, None, backward=True, pixels=pixels, own=own)
    total = all_sum(grad)
    recon = run_half(shifts, other, field, None, weights, recon, backward=False, pixels=pixels, own=own)
    return (recon,) + unpack(total, bands, proj_weight.shape[0], enc_weight.shape[0])


def solution(mesh):
    in_specs = (P("rows", "cols"), P("rows", "cols"), P(), P(None, "rows", "cols"), P(), P(), P(), P())
    out_specs = (P("segment", "rows", "cols"), P(), P(), P(), P())
    return jax.shard_map(
        per_device, mesh=mesh, in_specs=in_specs, out_specs=out_specs, check_vma=False
    )
```

```python
import functools
import jax
import jax.numpy as jnp
from jax import lax
from jax.experimental import pallas as pl
from jax.experimental.pallas import tpu as pltpu
from jax.sharding import PartitionSpec as P

AXES = ("segment", "rows", "cols")
BP = 32
SLAB = 3 * BP
STEP = 8
GROWS = 896


def nt(x, y):
    return lax.dot_general(x, y, (((1,), (1,)), ((), ())), preferred_element_type=jnp.float32)


def mm(x, y):
    return jnp.dot(x, y, preferred_element_type=jnp.float32)


def onehot(shape, rule):
    row = lax.broadcasted_iota(jnp.int32, shape, 0)
    col = lax.broadcasted_iota(jnp.int32, shape, 1)
    return rule(row, col).astype(jnp.float32)


def pixel_kernel(
    shifts_ref, place_ref, field_ref, *refs,
    backward, half_rows, cols, bands, fine, chan, inv_pixels, own, rec_rows,
):
    if backward:
        (target_ref, wenc_ref, wproj_ref, wprojt_ref, win_ref, wout_ref, woutt_ref,
         recon_ref, grad_ref, x3, ibuf, mid, perm, back, gather, widen, patch, hid_s, rec_s,
         fold, slope_s, eslope_s, res_s, pg_s, gin) = refs
    else:
        (wenc_ref, wproj_ref, win_ref, wout_ref, _, recon_ref,
         x3, ibuf, mid, perm, back, gather, widen, patch, hid_s, rec_s) = refs
    step = pl.program_id(0)
    half = place_ref[0]
    first_band = place_ref[1]
    ext = cols + 128
    quart = cols // 4
    groups = cols // 512
    bf16, f32 = jnp.bfloat16, jnp.float32
    center = lambda slot: slice(slot * SLAB + BP, slot * SLAB + 2 * BP)

    def build(group, dest):
        start = pl.multiple_of(half * half_rows + STEP * group, STEP)
        tiles = ext // 128
        meas = [field_ref[0, pl.ds(start, STEP), 128 * t:128 * t + 128] for t in range(tiles)]
        aper = [field_ref[1, pl.ds(start, STEP), 128 * t:128 * t + 128] for t in range(tiles)]
        lane = lax.broadcasted_iota(jnp.int32, (STEP, 128), 1)
        for k in range(0, bands, 2):
            pair = []
            for kk in (k, k + 1):
                s = shifts_ref[kk]
                keep = lane < 128 - s
                turned = [pltpu.roll(m, jnp.where(s == 0, 0, 128 - s), 1) for m in meas]
                pair.append([jnp.where(keep, turned[t], turned[(t + 1) % tiles]) * aper[t] for t in range(tiles)])
            for t in range(tiles):
                ibuf[STEP * k:STEP * k + 2 * STEP, 128 * t:128 * t + 128] = jnp.concatenate(
                    [pair[0][t], pair[1][t]], axis=0).astype(bf16)
        for c in range(0, ext, 256):
            w = min(256, ext - c)
            mid[:, c:c + w] = mm(perm[...], ibuf[:, c:c + w]).astype(bf16)
        for r, slot in dest:
            rows = mid[r * BP:(r + 1) * BP, :]
            x3[slot * SLAB:slot * SLAB + BP, :] = pltpu.roll(rows, 1, 1)[:, :cols]
            x3[center(slot), :] = rows[:, :cols]
            x3[slot * SLAB + 2 * BP:(slot + 1) * SLAB, :] = pltpu.roll(rows, ext - 1, 1)[:, :cols]

    @pl.when(step == 0)
    def _():
        perm[...] = onehot(perm.shape, lambda i, j: (j == (i % BP) * STEP + i // BP) & (i % BP < bands)).astype(bf16)
        if backward:
            back[...] = onehot(back.shape, lambda i, j: j == (i % STEP) * BP + first_band + i // STEP).astype(bf16)
        else:
            back[...] = onehot(back.shape, lambda i, j: j == (i % STEP) * rec_rows + i // STEP).astype(bf16)
        gather[...] = onehot((512, 512), lambda i, j: i == 4 * (j % 128) + j // 128).astype(bf16)
        widen[...] = (0.5 * onehot((128, 512), lambda i, j: i == j // 4)).astype(bf16)
        if backward:
            fold[...] = onehot((512, 128), lambda i, j: i // 4 == j).astype(bf16)
            grad_ref[...] = jnp.zeros_like(grad_ref)
            gin[...] = jnp.zeros_like(gin)
        build(0, ((6, 0), (7, 1)))

    @pl.when(step > 0)
    def _():
        x3[0:2 * SLAB, :] = x3[STEP * SLAB:(STEP + 2) * SLAB, :]

    build(step + 1, tuple((r, r + 2) for r in range(STEP)))

    lhs = jnp.concatenate(
        [x3[center(1 + i), 512 * cg:512 * cg + 512] for cg in range(groups) for i in range(STEP)], axis=0)
    for n in range(0, 512, 256):
        out = mm(lhs, gather[:, n:n + 256]).astype(bf16)
        for cg in range(groups):
            for cr in range(2):
                for b in range(n // 128, n // 128 + 2):
                    patch[b * 4 * BP:(b + 1) * 4 * BP, cr * quart + 128 * cg:cr * quart + 128 * cg + 128] = (
                        out[cg * 8 * BP + cr * 4 * BP:cg * 8 * BP + (cr + 1) * 4 * BP, 128 * b - n:128 * b - n + 128])
    u = mm(wenc_ref[...], patch[...])
    t = jnp.tanh(u)
    ut = u * t
    feat = (u + ut).astype(bf16)
    if backward:
        eslope_s[...] = (1.0 + t) * ((1.0 + u) - ut)
    proj = mm(wproj_ref[...], feat).astype(bf16)

    for cr in range(2):
        for cg in range(groups):
            q0 = cr * quart + 128 * cg
            block = proj[:, q0:q0 + 128]
            weight = jnp.concatenate([jnp.concatenate([block] * 4, axis=0), win_ref[...]], axis=1)
            lanes = slice(512 * cg, 512 * cg + 512)
            data = jnp.concatenate([widen[...], x3[4 * cr * SLAB:(4 * cr + 6) * SLAB, lanes]], axis=0)
            u = mm(weight, data)
            t = jnp.tanh(u)
            ut = u * t
            rows = slice(cr * 4 * fine, (cr + 1) * 4 * fine)
            hid_s[rows, lanes] = (u + ut).astype(bf16)
            if backward:
                slope_s[rows, lanes] = (1.0 + t) * ((1.0 + u) - ut)

    for c in range(0, cols, 256):
        lanes = slice(c, c + 256)
        if backward:
            truth = mm(perm[...], target_ref[:, :, lanes].reshape(bands * STEP, 256))
        for r in range(STEP):
            data = jnp.concatenate([hid_s[r * fine:(r + 1) * fine, lanes], x3[center(r + 1), lanes]], axis=0)
            rec = mm(wout_ref[...], data).astype(bf16)
            rec_s[r * rec_rows:(r + 1) * rec_rows, lanes] = rec
            if backward:
                res_s[r * BP:(r + 1) * BP, lanes] = (rec.astype(f32) - truth[r * BP:(r + 1) * BP]).astype(bf16)
        image = mm(back[...], rec_s[:, lanes])
        recon_ref[:, :, lanes] = image.reshape(own, STEP, 256).astype(bf16)

    if backward:
        for r in range(STEP):
            rows = slice(r * fine, (r + 1) * fine)
            for c in range(0, cols, 256):
                lanes = slice(c, c + 256)
                hgrad = mm(woutt_ref[...], res_s[r * BP:(r + 1) * BP, lanes])
                pg_s[rows, lanes] = (hgrad * slope_s[rows, lanes]).astype(bf16)
        side = lambda ref, n: jnp.concatenate([ref[r * n:(r + 1) * n, :] for r in range(STEP)], axis=1)
        grad_ref[848:848 + BP, 0:fine] += nt(side(res_s, BP), side(hid_s, fine))
        gin[...] += nt(
            jnp.concatenate([x3[0:6 * SLAB, :], x3[4 * SLAB:10 * SLAB, :]], axis=1),
            jnp.concatenate([pg_s[0:4 * fine, :], pg_s[4 * fine:8 * fine, :]], axis=1))
        stack = jnp.concatenate([pg_s[:, 512 * cg:512 * cg + 512] for cg in range(groups)], axis=0)
        tot = mm(stack, fold[...])
        parts = []
        for cr in range(2):
            for cg in range(groups):
                o = cg * 8 * fine + cr * 4 * fine
                parts.append(tot[o:o + fine] + tot[o + fine:o + 2 * fine]
                             + tot[o + 2 * fine:o + 3 * fine] + tot[o + 3 * fine:o + 4 * fine])
        cadj = jnp.concatenate(parts, axis=1).astype(bf16)
        grad_ref[512:512 + fine, :] += nt(cadj, feat)
        fg = mm(wprojt_ref[...], cadj).astype(bf16)
        egp = (fg.astype(f32) * eslope_s[...]).astype(bf16)
        grad_ref[0:512, :] += nt(patch[...], egp)

        @pl.when(step == pl.num_programs(0) - 1)
        def _():
            for a in range(3):
                tap = gin[a * SLAB:(a + 1) * SLAB, 0:fine]
                for r in range(1, 4):
                    tap = tap + gin[(a + r) * SLAB:(a + r + 1) * SLAB, r * fine:(r + 1) * fine]
                grad_ref[560 + a * SLAB:560 + (a + 1) * SLAB, 0:fine] = tap
            grad_ref[...] = grad_ref[...] * inv_pixels


def run_half(shifts, place, field, target, weights, recon, *, backward, pixels, own):
    rows2, ext = field.shape[1:]
    cols = ext - 128
    tile_rows = rows2 - STEP
    half_rows = tile_rows // 2
    bands = shifts.shape[0]
    wenc, wproj, wprojt, win, wout, woutt, wout_own = weights
    chan, fine = wenc.shape[0], wproj.shape[0]
    steps = half_rows // STEP
    whole = lambda shape: pl.BlockSpec(shape, lambda i, *_: (0,) * len(shape))
    strip = lambda n: pl.BlockSpec((n, STEP, cols), lambda i, sh, pc: (0, pc[0] * steps + i, 0))
    f32, bf16 = jnp.float32, jnp.bfloat16
    rec_rows = BP if backward else wout_own.shape[0]
    vmem = pltpu.VMEM
    scratch = [vmem(((STEP + 2) * SLAB, cols), bf16), vmem((bands * STEP, ext), bf16), vmem((STEP * BP, ext), bf16),
               vmem((STEP * BP, bands * STEP), bf16), vmem((own * STEP, STEP * rec_rows), bf16),
               vmem((512, 512), bf16), vmem((128, 512), bf16), vmem((16 * BP, cols // 2), bf16),
               vmem((STEP * fine, cols), bf16), vmem((STEP * rec_rows, cols), bf16)]
    recon_shape = jax.ShapeDtypeStruct((own, tile_rows, cols), bf16)
    body = functools.partial(
        pixel_kernel, backward=backward, half_rows=half_rows, cols=cols, bands=bands, fine=fine,
        chan=chan, inv_pixels=1.0 / pixels, own=own, rec_rows=rec_rows)
    if backward:
        ops = (field, target, wenc, wproj, wprojt, win, wout, woutt)
        in_specs = [whole(field.shape), strip(bands)] + [whole(x.shape) for x in ops[2:]]
        out_shape = (recon_shape, jax.ShapeDtypeStruct((GROWS, 128), f32))
        out_specs = (strip(own), whole((GROWS, 128)))
        scratch += [vmem((512, 128), bf16), vmem((STEP * fine, cols), f32), vmem((chan, cols // 2), f32),
                    vmem((STEP * BP, cols), bf16), vmem((STEP * fine, cols), bf16), vmem((6 * SLAB, 4 * fine), f32)]
        alias = {}
    else:
        ops = (field, wenc, wproj, win, wout_own, recon)
        in_specs = [whole(x.shape) for x in ops[:5]] + [pl.BlockSpec(memory_space=pl.ANY)]
        out_shape = recon_shape
        out_specs = strip(own)
        alias = {7: 0}
    return pl.pallas_call(
        body,
        out_shape=out_shape,
        grid_spec=pltpu.PrefetchScalarGridSpec(
            num_scalar_prefetch=2, grid=(steps,), in_specs=in_specs, out_specs=out_specs,
            scratch_shapes=scratch),
        compiler_params=pltpu.CompilerParams(
            dimension_semantics=("arbitrary",), vmem_limit_bytes=56 << 20),
        input_output_aliases=alias,
        name="grad_half" if backward else "recon_half",
    )(shifts, place, *ops)


def moved(x, axis, by):
    n = lax.axis_size(axis)
    return lax.ppermute(x, axis, [(i, i + by) for i in range(n) if 0 <= i + by < n])


def bordered(measure, aperture):
    pair = jnp.stack([measure, aperture.astype(jnp.bfloat16)])
    right = moved(pair[:, :, :64], "cols", -1)
    left = moved(pair[:, :, -64:], "cols", 1)
    wide = jnp.concatenate([pair, right, left], axis=2)
    above = moved(wide[:, -8:], "rows", 1)
    below = moved(wide[:, :8], "rows", -1)
    return jnp.concatenate([above[:, 1:], wide, below[:, :1]], axis=1).astype(jnp.float32)


def pack_weights(enc_weight, proj_weight, in_weight, out_weight, first, own):
    bands, fine = out_weight.shape
    pad = BP - bands
    bf16 = jnp.bfloat16
    half = jnp.asarray(0.5, bf16)
    enc = jnp.pad(enc_weight.transpose(0, 3, 2, 1), ((0, 0), (0, 0), (0, 0), (0, pad)))
    enc = enc.reshape(enc.shape[0], -1) * half
    inw = jnp.pad(in_weight.transpose(2, 0, 1, 3), ((0, 0), (0, 0), (0, 0), (0, pad)))
    inw = inw.reshape(fine, -1) * half
    inw = jnp.concatenate([jnp.pad(inw, ((0, 0), (SLAB * r, SLAB * (3 - r)))) for r in range(4)], axis=0)
    out = jnp.pad(out_weight, ((0, pad), (0, 0)))
    head = jnp.concatenate([out, jnp.eye(BP, dtype=bf16)], axis=1)
    own_pad = -(-own // 16) * 16
    mine = lax.dynamic_slice_in_dim(head, first, own, 0)
    mine = jnp.pad(mine, ((0, own_pad - own), (0, 0)))
    return enc, proj_weight, proj_weight.T * half, inw, head, out.T * half, mine


def unpack(total, bands, fine, chan):
    enc = total[:512].reshape(4, 4, BP, chan)[:, :, :bands].transpose(3, 2, 1, 0)
    proj = total[512:512 + fine]
    gin = total[560:560 + 9 * BP, :fine].reshape(3, 3, BP, fine)[:, :, :bands].transpose(0, 1, 3, 2)
    out = total[848:848 + bands, :fine]
    return enc, proj, gin, out


def all_sum(grad):
    n = lax.axis_size(AXES)
    mine = lax.all_to_all(grad.reshape(n, GROWS // n, 128), AXES, 0, 0, tiled=True)
    mine = jnp.sum(mine, axis=0)
    every = lax.all_to_all(jnp.broadcast_to(mine, (n,) + mine.shape), AXES, 0, 0, tiled=True)
    return every.reshape(GROWS, 128)


def per_device(measure, aperture, shifts, target, enc_weight, proj_weight, in_weight, out_weight):
    tile_rows, tile_cols = measure.shape
    bands = shifts.shape[0]
    pixels = float(tile_rows * lax.axis_size("rows") * tile_cols * lax.axis_size("cols"))
    seg = lax.axis_index("segment")
    own = bands // lax.axis_size("segment")
    field = bordered(measure, aperture)
    weights = pack_weights(enc_weight, proj_weight, in_weight, out_weight, seg * own, own)
    place = jnp.stack([seg, seg * own]).astype(jnp.int32)
    other = jnp.stack([1 - seg, seg * own]).astype(jnp.int32)
    recon, grad = run_half(shifts, place, field, target, weights, None, backward=True, pixels=pixels, own=own)
    total = all_sum(grad)
    recon = run_half(shifts, other, field, None, weights, recon, backward=False, pixels=pixels, own=own)
    return (recon,) + unpack(total, bands, proj_weight.shape[0], enc_weight.shape[0])


def solution(mesh):
    in_specs = (P("rows", "cols"), P("rows", "cols"), P(), P(None, "rows", "cols"), P(), P(), P(), P())
    out_specs = (P("segment", "rows", "cols"), P(), P(), P(), P())
    return jax.shard_map(
        per_device, mesh=mesh, in_specs=in_specs, out_specs=out_specs, check_vma=False
    )
```
